128 devices in a mesh: dp: 8 (over y, core), expert: 16 (over z, x).
Axes of the slice: x: 4, y: 4, z: 4, core: 2. Of those that a mesh axis runs over, the one named last changes fastest.
Arguments:
- tokens: bfloat16 [16384, 4096], P(('dp', 'expert')), may hold values from -6 to 6
- router_weights: float32 [16384, 8], P(('dp', 'expert')), may hold values from 0.1 to 1
- expert_ids: int32 [16384, 8], P(('dp', 'expert')), may hold values from 0 to 127, as said below
- gate_weight: bfloat16 [128, 4096, 768], P(('dp', 'expert')), may hold values from -0.09375 to 0.09375
- up_weight: bfloat16 [128, 4096, 768], P(('dp', 'expert')), may hold values from -0.09375 to 0.09375
- down_weight: bfloat16 [128, 768, 4096], P(('dp', 'expert')), may hold values from -0.21875 to 0.21875
Outputs:
- mixed: bfloat16 [16384, 4096], P(('dp', 'expert'))
The draws below stay inside these ranges and needn't reach their ends.
Inputs may be any that keep to these rules, and one draw needn't show every extreme that they name: `expert_ids`: each row names 8 different experts. Experts e and e + 16 with e // 16 even form a pair: the 128 tokens of one device (aligned blocks of rows) name the two experts of each pair exactly 2 * 8 times together, and one expert at most 12 times; some expert is named exactly 12 times by the tokens of every device.
All inputs are finite; a program needn't handle non-finite values.
Results may differ from the reference program's by a relative error of at most 0.0058.
Values may be sent and summed in bfloat16 or wider, within the bound.
A program may use at most 192 MiB of HBM per device.

```python
from functools import partial
import jax
import jax.numpy as jnp
from jax import lax

D = 4096
FF = 768
TOP = 8
TOK_DEV = 128
EXPERTS = 128
GROUP = 16
TOKENS = 16384
MOST = 12


def permute_range(one_key, size):
    return jax.random.permutation(one_key, size).astype(jnp.int32)


def draw_expert_ids(key, part):
    pair_count = EXPERTS // 2
    slot_cap = TOK_DEV * TOP // EXPERTS
    key_list = jax.random.split(key, 7)
    pair_order = jax.vmap(partial(permute_range, size=pair_count))(jax.random.split(key_list[0], EXPERTS))
    rank_table = jax.vmap(partial(permute_range, size=2 * slot_cap))(jax.random.split(key_list[1], EXPERTS * pair_count))
    rank_table = rank_table.reshape(EXPERTS, pair_count, 2 * slot_cap)
    slot_index = jnp.arange(TOK_DEV * TOP, dtype=jnp.int32)
    column = slot_index % pair_count
    occurrence = slot_index // pair_count
    pair = pair_order[:, column]
    hot_pair = jax.random.randint(key_list[2], (pair_count,), 0, 4) == 0
    full_pair = jax.random.randint(key_list[3], (), 0, pair_count)
    cold = jax.random.randint(key_list[4], (EXPERTS, pair_count), slot_cap - slot_cap // 4, slot_cap + slot_cap // 4 + 1)
    warm = jax.random.randint(key_list[5], (EXPERTS, pair_count), 5 * slot_cap // 4, 3 * slot_cap // 2 + 1)
    side_count = jnp.where(hot_pair[None, :], warm, cold)
    side_count = jnp.where(jnp.arange(pair_count)[None, :] == full_pair, 3 * slot_cap // 2, side_count)
    flip = jax.random.randint(key_list[6], (pair_count,), 0, 2)
    sources = jnp.arange(EXPERTS, dtype=jnp.int32)[:, None]
    rank_value = rank_table[sources, pair, occurrence[None, :]]
    count_here = side_count[sources, pair]
    is_high = jnp.where(rank_value < count_here, 1, 0)
    is_high = jnp.where(flip[pair] == 1, 1 - is_high, is_high)
    low_expert = pair // GROUP * 2 * GROUP + pair % GROUP
    chosen = low_expert + GROUP * is_high
    return chosen.reshape(TOKENS, TOP).astype(jnp.int32)


def steps_of(stream_key, dims, shards, least, high):
    factor_of = 1.0
    for axis_at, parts in shards:
        steps = jax.random.uniform(jax.random.fold_in(jax.random.fold_in(stream_key, 6), axis_at), (parts,), jnp.float32, least / len(shards), high / len(shards))
        factor_of = factor_of * jnp.repeat(jnp.exp(steps), dims[axis_at] // parts).reshape((-1,) + (1,) * (len(dims) - 1 - axis_at))
    return factor_of


def bell_draw(key, dims, spread, bound, shards=(), kind=jnp.bfloat16):
    values = spread * jax.random.normal(key, dims, jnp.float32)
    if shards:
        values = values * steps_of(key, dims, shards, -0.22, 0.18)
    return jnp.clip(values, -bound, bound).astype(kind)


def setup_inputs(seed: int = 0) -> dict:
    arg_keys = jax.random.split(jax.random.key(seed), 7)
    return {
        "tokens": bell_draw(arg_keys[0], (TOKENS, D), 1.0, 6.0, ((0, 128),)),
        "router_weights": jnp.clip(0.1 + 0.9 * jax.random.uniform(arg_keys[1], (TOKENS, TOP), jnp.float32) ** steps_of(arg_keys[1], (TOKENS, TOP), ((0, 128),), -0.2, 0.2), 0.1, 1.0),
        "expert_ids": draw_expert_ids(jax.random.fold_in(arg_keys[6], 71), 0),
        "gate_weight": bell_draw(arg_keys[3], (EXPERTS, D, FF), D ** -0.5, 0.09375, ((0, 128),)),
        "up_weight": bell_draw(arg_keys[4], (EXPERTS, D, FF), D ** -0.5, 0.09375, ((0, 128),)),
        "down_weight": bell_draw(arg_keys[5], (EXPERTS, FF, D), FF ** -0.5, 0.21875, ((0, 128),)),
    }


def reference(tokens, router_weights, expert_ids, gate_weight, up_weight, down_weight):
    most_rows = MOST * EXPERTS
    flat_ids = expert_ids.reshape(-1).astype(jnp.int32)
    ordering = jnp.argsort(flat_ids, stable=True).astype(jnp.int32)
    counts = jnp.sum((flat_ids[:, None] == jnp.arange(EXPERTS, dtype=jnp.int32)[None, :]).astype(jnp.int32), axis=0)
    starts = (jnp.cumsum(counts) - counts).astype(jnp.int32)
    padded = jnp.concatenate([ordering, jnp.zeros((most_rows,), jnp.int32)])
    flat_gates = router_weights.reshape(-1)

    def per_expert(summed, expert):
        picked = lax.dynamic_slice_in_dim(padded, starts[expert], most_rows)
        is_valid = jnp.arange(most_rows, dtype=jnp.int32) < counts[expert]
        row_data = tokens[picked // TOP]
        gate_proj = jnp.dot(row_data, gate_weight[expert], preferred_element_type=jnp.float32)
        up_proj = jnp.dot(row_data, up_weight[expert], preferred_element_type=jnp.float32)
        hidden = (jax.nn.silu(gate_proj) * up_proj).astype(jnp.bfloat16)
        result = jnp.dot(hidden, down_weight[expert], preferred_element_type=jnp.float32).astype(jnp.bfloat16)
        weight = jnp.where(is_valid, flat_gates[picked], jnp.zeros_like(flat_gates[picked]))
        summed = summed.at[picked // TOP].add(weight[:, None] * result.astype(jnp.float32))
        return summed, None

    summed, unused = lax.scan(per_expert, jnp.zeros((TOKENS, D), jnp.float32), jnp.arange(EXPERTS, dtype=jnp.int32))
    return summed.astype(jnp.bfloat16)
```

```python
import jax
import jax.numpy as jnp
import itertools
from jax import lax
from jax.experimental import pallas as pl
from jax.experimental.pallas import tpu as pltpu
from jax.sharding import PartitionSpec as P

MESH = pl.DeviceIdType.MESH
F32 = jnp.float32
BF16 = jnp.bfloat16
D = 4096
FF = 768
CHIPS = 64
GS = 16
NG = CHIPS // GS
CT = 512
NT = D // CT


def balanced_order():
    every = list(itertools.product(range(4), repeat=3))
    left = set(every[1:])
    order = [every[0]]
    kinds = sorted(itertools.product(range(3), repeat=3), key=lambda t: (-t.count(1), t))
    for kind in kinds:
        ones = [i for i in range(3) if kind[i] == 1]
        twin = tuple(2 - d for d in kind)
        for signs in itertools.product((1, 3), repeat=len(ones)):
            flipped = tuple(4 - s for s in signs)
            for base, sg in ((kind, signs), (twin, flipped), (kind, flipped), (twin, signs)):
                offset = list(base)
                for i, s in zip(ones, sg):
                    offset[i] = s
                offset = tuple(offset)
                if offset in left:
                    left.remove(offset)
                    order.append(offset)
    return order


ORDER = balanced_order()
WORDS = [
    [sum(ORDER[8 * b + j][axis] * 4**j for j in range(8)) for b in range(8)] for axis in range(3)
]


def pick_word(b, words):
    value = jnp.int32(words[0])
    for k in range(1, 8):
        value = jnp.where(b == k, jnp.int32(words[k]), value)
    return value


def offsets_of(b):
    found = [pick_word(b, WORDS[axis]) for axis in range(3)]
    return [tuple(lax.rem(lax.div(w, jnp.int32(4**j)), jnp.int32(4)) for w in found) for j in range(8)]


def kernel(
    tok_hbm, ids_ref, rw_ref, wg_hbm, wu_hbm, wd_hbm,
    out_ref,
    tok, aux, auxs, cnt, meta, onehot, send, arr, pmix, pout, ret,
    wg, wu, wd, xs, hid, comb, acc, part,
    in_sem, wt_sem, start_s, start_r, meta_s, meta_r, disp_s, disp_r, ret_s, ret_r,
    mix_s, mix_r, po_s, po_r, part_s, part_r,
):
    dp = lax.axis_index("dp")
    ex = lax.axis_index("expert")
    y, c = dp // 2, dp % 2
    z, x = ex // 4, ex % 4
    partner = (y * 2 + (1 - c), ex)

    def chip_at(o, sign):
        dx, dy, dz = o
        xx = lax.rem(x + (dx if sign > 0 else 4 - dx), 4)
        yy = lax.rem(y + (dy if sign > 0 else 4 - dy), 4)
        zz = lax.rem(z + (dz if sign > 0 else 4 - dz), 4)
        return xx, yy, zz

    def device_at(o, sign):
        xx, yy, zz = chip_at(o, sign)
        return (yy * 2 + c, zz * 4 + xx)

    def pair_at(o):
        xx, yy, zz = chip_at(o, 1)
        return yy * 16 + zz * 4 + xx

    tok_in = pltpu.make_async_copy(tok_hbm, tok.at[c], in_sem)
    tok_in.start()
    w_in = [
        pltpu.make_async_copy(src, dst, wt_sem.at[i])
        for i, (src, dst) in enumerate(((wg_hbm, wg), (wu_hbm, wu), (wd_hbm, wd)))
    ]
    for copy in w_in:
        copy.start()

    barrier = pltpu.get_barrier_semaphore()
    pl.semaphore_signal(barrier, inc=1, device_id=partner, device_id_type=MESH)

    def greet(i, carry):
        other = device_at((i // 16, (i // 4) % 4, i % 4), 1)
        pl.semaphore_signal(barrier, inc=1, device_id=other, device_id_type=MESH)
        return carry

    lax.fori_loop(1, CHIPS, greet, 0)

    expert_io = lax.broadcasted_iota(jnp.int32, (128, 128), 0)
    named = jnp.zeros((128, 128), F32)
    weight = jnp.zeros((128, 128), F32)
    for k in range(8):
        hit = expert_io == ids_ref[k : k + 1, :]
        named = named + jnp.where(hit, 1.0, 0.0)
        weight = weight + jnp.where(hit, rw_ref[k : k + 1, :], 0.0)
    t_from = lax.broadcasted_iota(jnp.int32, (128, 128), 0)
    t_to = lax.broadcasted_iota(jnp.int32, (128, 128), 1)
    before = jnp.where(t_from < t_to, 1.0, 0.0).astype(BF16)
    rank = jnp.dot(named.astype(BF16), before, preferred_element_type=F32)
    counts = lax.dot_general(
        jnp.ones((8, 128), BF16), named.astype(BF16), (((1,), (1,)), ((), ())),
        preferred_element_type=F32,
    )

    def side(values, low):
        return jnp.concatenate(
            [values[32 * k + 16 * low : 32 * k + 16 * low + 16] for k in range(4)], axis=0
        )

    named2 = [side(named, 0), side(named, 1)]
    weight2 = [side(weight, 0), side(weight, 1)]
    rank2 = [side(rank, 0), side(rank, 1)]
    shift = (4 * c).astype(F32)

    def view(own, other):
        q_own = rank2[own]
        row_own = jnp.where(
            (named2[own] > 0.5) & (q_own < 7.5), q_own + jnp.where(q_own > 3.5, 4.0, 0.0) + shift, -1.0
        )
        q_other = 15.0 - rank2[other]
        row_other = jnp.where((named2[other] > 0.5) & (q_other < 7.5), q_other + 4.0 + shift, -1.0)
        return row_own, row_other, weight2[own], weight2[other]

    views = (view(0, 1), view(1, 0))
    for k in range(4):
        aux[c, k] = jnp.where(c == 0, views[0][k], views[1][k])
        auxs[k] = jnp.where(c == 0, views[1][k], views[0][k])
    cnt[c] = counts[0:1, :]

    pl.semaphore_wait(barrier, CHIPS)

    starts = [
        pltpu.make_async_remote_copy(
            src, dst, start_s.at[i], start_r.at[i], device_id=partner, device_id_type=MESH
        )
        for i, (src, dst) in enumerate(
            ((auxs, aux.at[c]), (cnt.at[c], cnt.at[c]), (tok_hbm, tok.at[c]))
        )
    ]
    for copy in starts:
        copy.start()
    tok_in.wait()
    for copy in starts:
        copy.wait()

    meta[0] = cnt[...]

    def meta_copy(i, o):
        return pltpu.make_async_remote_copy(
            cnt, meta.at[i], meta_s.at[i], meta_r.at[i],
            device_id=device_at(o, 1), device_id_type=MESH,
        )

    def send_copy(i, o):
        return pltpu.make_async_remote_copy(
            send.at[i], arr.at[i], disp_s.at[i], disp_r.at[i],
            device_id=device_at(o, 1), device_id_type=MESH,
        )

    def ret_copy(i, o):
        return pltpu.make_async_remote_copy(
            arr.at[i], ret.at[i], ret_s.at[i], ret_r.at[i],
            device_id=device_at(o, -1), device_id_type=MESH,
        )

    row_io = lax.broadcasted_iota(jnp.int32, (16, 256), 0).astype(F32)

    def aux_row(k, pair):
        return jnp.concatenate(
            [aux[0, k, pl.ds(pair, 1), :], aux[1, k, pl.ds(pair, 1), :]], axis=1
        )

    def dispatch(b, carry):
        offs = offsets_of(b)
        for j in range(8):
            pair = pair_at(offs[j])
            hit = (row_io == aux_row(0, pair)) | (row_io == aux_row(1, pair))
            onehot[16 * j : 16 * j + 16, :] = jnp.where(hit, 1.0, 0.0).astype(BF16)

        def tile(n, inner):
            cols = pl.ds(pl.multiple_of(n * CT, CT), CT)
            rows = jnp.dot(
                onehot[...], tok[:, :, cols].reshape(256, CT), preferred_element_type=F32
            )
            send[pl.ds(b * 8, 8), :, :, cols] = rows.reshape(8, 2, 8, CT).astype(BF16)
            return inner

        lax.fori_loop(0, NT, tile, 0)
        for j in range(8):
            i = b * 8 + j

            def go(i=i, j=j):
                meta_copy(i, offs[j]).start()
                send_copy(i, offs[j]).start()

            if j == 0:
                pl.when(b > 0)(go)
            else:
                go()
        return carry

    lax.fori_loop(0, 8, dispatch, 0)
    arr[0] = send[0]

    for copy in w_in:
        copy.wait()

    me_lane = dp * 16 + ex
    lane_io = lax.broadcasted_iota(jnp.int32, (1, 1, 1, 128), 3)
    mix_row = lax.broadcasted_iota(jnp.int32, (GS, 8, 1), 1)

    def experts(g, carry):
        chunk = pl.ds(g * GS, GS)

        def arrived(i, inner):
            @pl.when(i > 0)
            def _():
                meta_copy(i, (0, 0, 0)).wait_recv()
                send_copy(i, (0, 0, 0)).wait_recv()

            return inner

        lax.fori_loop(g * GS, g * GS + GS, arrived, 0)
        mix = pltpu.make_async_remote_copy(
            arr.at[chunk, 1], pmix.at[chunk], mix_s.at[g], mix_r.at[g],
            device_id=partner, device_id_type=MESH,
        )
        mix.start()

        def load_own(n, inner):
            cols = pl.ds(pl.multiple_of(n * CT, CT), CT)
            xs[0 : GS * 16, cols] = arr[chunk, :, :, cols].astype(F32).reshape(GS * 16, CT).astype(BF16)
            return inner

        lax.fori_loop(0, NT, load_own, 0)
        mix.wait()

        def load_mix(n, inner):
            cols = pl.ds(pl.multiple_of(n * CT, CT), CT)
            xs[GS * 16 : GS * 24, cols] = pmix[chunk, :, cols].astype(F32).reshape(GS * 8, CT).astype(BF16)
            return inner

        lax.fori_loop(0, NT, load_mix, 0)

        def hidden(n, inner):
            cols = pl.ds(pl.multiple_of(n * 256, 256), 256)
            gate = jnp.dot(xs[...], wg[:, cols], preferred_element_type=F32)
            up = jnp.dot(xs[...], wu[:, cols], preferred_element_type=F32)
            hid[:, cols] = (gate / (1.0 + jnp.exp(-gate)) * up).astype(BF16)
            return inner

        lax.fori_loop(0, FF // 256, hidden, 0)

        def down(n, inner):
            cols = pl.ds(pl.multiple_of(n * CT, CT), CT)
            rows = jnp.dot(hid[...], wd[:, cols], preferred_element_type=F32)
            arr[chunk, :, :, cols] = rows[0 : GS * 16].reshape(GS, 2, 8, CT).astype(BF16)
            pmix[chunk, :, cols] = rows[GS * 16 :].reshape(GS, 8, CT).astype(BF16)
            return inner

        lax.fori_loop(0, NT, down, 0)
        back = pltpu.make_async_remote_copy(
            pmix.at[chunk], pout.at[chunk], po_s.at[g], po_r.at[g],
            device_id=partner, device_id_type=MESH,
        )
        back.start()
        found = jnp.sum(jnp.where(lane_io == me_lane, meta[chunk], 0.0), axis=3, keepdims=True)
        own0, own1 = found[:, 0], found[:, 1]
        bound = jnp.where(mix_row < 4, own0, own1)
        mine = (4 + lax.rem(mix_row, 4)).astype(F32) < bound
        back.wait()

        def choose(n, inner):
            cols = pl.ds(pl.multiple_of(n * CT, CT), CT)
            own = arr[chunk, 1, :, cols].astype(F32)
            other = pout[chunk, :, cols].astype(F32)
            arr[chunk, 1, :, cols] = jnp.where(mine, own, other).astype(BF16)
            return inner

        lax.fori_loop(0, NT, choose, 0)
        for h in range(GS // 8):
            offs = offsets_of(g * (GS // 8) + h)
            for j in range(8):
                i = g * GS + h * 8 + j

                def go(i=i, o=offs[j]):
                    ret_copy(i, o).start()

                if h == 0 and j == 0:
                    pl.when(g > 0)(go)
                else:
                    go()
        return carry

    lax.fori_loop(0, NG, experts, 0)
    ret[0] = arr[0]
    acc[...] = jnp.zeros_like(acc)

    def combine(g, carry):
        def arrived(i, inner):
            @pl.when(i > 0)
            def _():
                ret_copy(i, (0, 0, 0)).wait_recv()

            return inner

        lax.fori_loop(g * GS, g * GS + GS, arrived, 0)
        blocks = []
        for h in range(GS // 8):
            offs = offsets_of(g * (GS // 8) + h)
            for j in range(8):
                pair = pair_at(offs[j])
                blocks.append(
                    jnp.where(row_io == aux_row(0, pair), aux_row(2, pair), 0.0)
                    + jnp.where(row_io == aux_row(1, pair), aux_row(3, pair), 0.0)
                )
        mixer = jnp.transpose(jnp.concatenate(blocks, axis=0))
        high = mixer.astype(BF16)
        comb[0:256, :] = high
        comb[256:512, :] = (mixer - high.astype(F32)).astype(BF16)

        def tile(n, inner):
            cols = pl.ds(pl.multiple_of(n * CT, CT), CT)
            rows = ret[pl.ds(g * GS, GS), :, :, cols].astype(F32).reshape(GS * 16, CT).astype(BF16)
            both = jnp.dot(comb[...], rows, preferred_element_type=F32)
            acc[:, :, cols] += (both[0:256] + both[256:512]).reshape(2, 128, CT)
            return inner

        lax.fori_loop(0, NT, tile, 0)
        return carry

    lax.fori_loop(0, NG, combine, 0)

    def part_copy(n):
        cols = pl.ds(pl.multiple_of(n * CT, CT), CT)
        return pltpu.make_async_remote_copy(
            acc.at[1 - c, :, cols], part.at[:, cols], part_s.at[n], part_r.at[n],
            device_id=partner, device_id_type=MESH,
        )

    def part_go(n, carry):
        part_copy(n).start()
        return carry

    lax.fori_loop(0, NT, part_go, 0)

    def finish(n, carry):
        cols = pl.ds(pl.multiple_of(n * CT, CT), CT)
        part_copy(n).wait_recv()
        out_ref[:, cols] = (acc[c, :, cols] + part[:, cols]).astype(BF16)
        return carry

    lax.fori_loop(0, NT, finish, 0)

    def drain(i, carry):
        meta_copy(i, (0, 0, 0)).wait_send()
        send_copy(i, (0, 0, 0)).wait_send()
        ret_copy(i, (0, 0, 0)).wait_send()
        return carry

    lax.fori_loop(1, CHIPS, drain, 0)

    def part_drain(n, carry):
        part_copy(n).wait_send()
        return carry

    lax.fori_loop(0, NT, part_drain, 0)


def local(tokens, router_weights, expert_ids, gate_weight, up_weight, down_weight):
    sem = pltpu.SemaphoreType.DMA
    hbm = pl.BlockSpec(memory_space=pl.ANY)
    vmem = pl.BlockSpec(memory_space=pltpu.VMEM)
    return pl.pallas_call(
        kernel,
        out_shape=jax.ShapeDtypeStruct((128, D), BF16),
        in_specs=[hbm, vmem, vmem, hbm, hbm, hbm],
        out_specs=vmem,
        scratch_shapes=[
            pltpu.VMEM((2, 128, D), BF16),
            pltpu.VMEM((2, 4, 64, 128), F32),
            pltpu.VMEM((4, 64, 128), F32),
            pltpu.VMEM((2, 1, 128), F32),
            pltpu.VMEM((CHIPS, 2, 1, 128), F32),
            pltpu.VMEM((128, 256), BF16),
            pltpu.VMEM((CHIPS, 2, 8, D), BF16),
            pltpu.VMEM((CHIPS, 2, 8, D), BF16),
            pltpu.VMEM((CHIPS, 8, D), BF16),
            pltpu.VMEM((CHIPS, 8, D), BF16),
            pltpu.VMEM((CHIPS, 2, 8, D), BF16),
            pltpu.VMEM((D, FF), BF16),
            pltpu.VMEM((D, FF), BF16),
            pltpu.VMEM((FF, D), BF16),
            pltpu.VMEM((GS * 24, D), BF16),
            pltpu.VMEM((GS * 24, FF), BF16),
            pltpu.VMEM((512, GS * 16), BF16),
            pltpu.VMEM((2, 128, D), F32),
            pltpu.VMEM((128, D), F32),
            sem, sem((3,)), sem((3,)), sem((3,)),
            sem((CHIPS,)), sem((CHIPS,)), sem((CHIPS,)), sem((CHIPS,)), sem((CHIPS,)), sem((CHIPS,)),
            sem((NG,)), sem((NG,)), sem((NG,)), sem((NG,)), sem((NT,)), sem((NT,)),
        ],
        compiler_params=pltpu.CompilerParams(
            collective_id=0, has_side_effects=True, vmem_limit_bytes=67043328
        ),
    )(
        tokens, expert_ids.T, router_weights.T,
        gate_weight[0], up_weight[0], down_weight[0],
    )


def solution(mesh):
    split = ("dp", "expert")
    return jax.shard_map(
        local,
        mesh=mesh,
        in_specs=(
            P(split, None), P(split, None), P(split, None),
            P(split, None, None), P(split, None, None), P(split, None, None),
        ),
        out_specs=P(split, None),
        check_vma=False,
    )
```

```python
import jax
import jax.numpy as jnp
import itertools
from jax import lax
from jax.experimental import pallas as pl
from jax.experimental.pallas import tpu as pltpu
from jax.sharding import PartitionSpec as P

MESH = pl.DeviceIdType.MESH
F32 = jnp.float32
BF16 = jnp.bfloat16
D = 4096
FF = 768
CHIPS = 64
GS = 16
NG = CHIPS // GS
CT = 512
NT = D // CT


def balanced_order():
    every = list(itertools.product(range(4), repeat=3))
    left = set(every[1:])
    order = [every[0]]
    kinds = sorted(itertools.product(range(3), repeat=3), key=lambda t: (-t.count(1), t))
    for kind in kinds:
        ones = [i for i in range(3) if kind[i] == 1]
        twin = tuple(2 - d for d in kind)
        for signs in itertools.product((1, 3), repeat=len(ones)):
            flipped = tuple(4 - s for s in signs)
            for base, sg in ((kind, signs), (twin, flipped), (kind, flipped), (twin, signs)):
                offset = list(base)
                for i, s in zip(ones, sg):
                    offset[i] = s
                offset = tuple(offset)
                if offset in left:
                    left.remove(offset)
                    order.append(offset)
    return order


ORDER = balanced_order()
WORDS = [
    [sum(ORDER[8 * b + j][axis] * 4**j for j in range(8)) for b in range(8)] for axis in range(3)
]


def pick_word(b, words):
    value = jnp.int32(words[0])
    for k in range(1, 8):
        value = jnp.where(b == k, jnp.int32(words[k]), value)
    return value


def offsets_of(b):
    found = [pick_word(b, WORDS[axis]) for axis in range(3)]
    return [tuple(lax.rem(lax.div(w, jnp.int32(4**j)), jnp.int32(4)) for w in found) for j in range(8)]


def kernel(
    tok_hbm, ids_ref, rw_ref, wg_hbm, wu_hbm, wd_hbm,
    out_ref,
    tok, aux, auxs, cnt, meta, onehot, send, arr, pmix, pout, ret,
    wg, wu, wd, xs, hid, comb, acc, part,
    in_sem, wt_sem, start_s, start_r, meta_s, meta_r, disp_s, disp_r, ret_s, ret_r,
    mix_s, mix_r, po_s, po_r, part_s, part_r,
):
    dp = lax.axis_index("dp")
    ex = lax.axis_index("expert")
    y, c = dp // 2, dp % 2
    z, x = ex // 4, ex % 4
    partner = (y * 2 + (1 - c), ex)

    def chip_at(o, sign):
        dx, dy, dz = o
        xx = lax.rem(x + (dx if sign > 0 else 4 - dx), 4)
        yy = lax.rem(y + (dy if sign > 0 else 4 - dy), 4)
        zz = lax.rem(z + (dz if sign > 0 else 4 - dz), 4)
        return xx, yy, zz

    def device_at(o, sign):
        xx, yy, zz = chip_at(o, sign)
        return (yy * 2 + c, zz * 4 + xx)

    def pair_at(o):
        xx, yy, zz = chip_at(o, 1)
        return yy * 16 + zz * 4 + xx

    tok_in = pltpu.make_async_copy(tok_hbm, tok.at[c], in_sem)
    tok_in.start()
    w_in = [
        pltpu.make_async_copy(src, dst, wt_sem.at[i])
        for i, (src, dst) in enumerate(((wg_hbm, wg), (wu_hbm, wu), (wd_hbm, wd)))
    ]
    for copy in w_in:
        copy.start()

    barrier = pltpu.get_barrier_semaphore()
    pl.semaphore_signal(barrier, inc=1, device_id=partner, device_id_type=MESH)

    def greet(i, carry):
        other = device_at((i // 16, (i // 4) % 4, i % 4), 1)
        pl.semaphore_signal(barrier, inc=1, device_id=other, device_id_type=MESH)
        return carry

    lax.fori_loop(1, CHIPS, greet, 0)

    expert_io = lax.broadcasted_iota(jnp.int32, (128, 128), 0)
    named = jnp.zeros((128, 128), F32)
    weight = jnp.zeros((128, 128), F32)
    for k in range(8):
        hit = expert_io == ids_ref[k : k + 1, :]
        named = named + jnp.where(hit, 1.0, 0.0)
        weight = weight + jnp.where(hit, rw_ref[k : k + 1, :], 0.0)
    t_from = lax.broadcasted_iota(jnp.int32, (128, 128), 0)
    t_to = lax.broadcasted_iota(jnp.int32, (128, 128), 1)
    before = jnp.where(t_from < t_to, 1.0, 0.0).astype(BF16)
    rank = jnp.dot(named.astype(BF16), before, preferred_element_type=F32)
    counts = lax.dot_general(
        jnp.ones((8, 128), BF16), named.astype(BF16), (((1,), (1,)), ((), ())),
        preferred_element_type=F32,
    )

    def side(values, low):
        return jnp.concatenate(
            [values[32 * k + 16 * low : 32 * k + 16 * low + 16] for k in range(4)], axis=0
        )

    named2 = [side(named, 0), side(named, 1)]
    weight2 = [side(weight, 0), side(weight, 1)]
    rank2 = [side(rank, 0), side(rank, 1)]
    shift = (4 * c).astype(F32)

    def view(own, other):
        q_own = rank2[own]
        row_own = jnp.where(
            (named2[own] > 0.5) & (q_own < 7.5), q_own + jnp.where(q_own > 3.5, 4.0, 0.0) + shift, -1.0
        )
        q_other = 15.0 - rank2[other]
        row_other = jnp.where((named2[other] > 0.5) & (q_other < 7.5), q_other + 4.0 + shift, -1.0)
        return row_own, row_other, weight2[own], weight2[other]

    views = (view(0, 1), view(1, 0))
    for k in range(4):
        aux[c, k] = jnp.where(c == 0, views[0][k], views[1][k])
        auxs[k] = jnp.where(c == 0, views[1][k], views[0][k])
    cnt[c] = counts[0:1, :]

    pl.semaphore_wait(barrier, CHIPS)

    starts = [
        pltpu.make_async_remote_copy(
            src, dst, start_s.at[i], start_r.at[i], device_id=partner, device_id_type=MESH
        )
        for i, (src, dst) in enumerate(
            ((auxs, aux.at[c]), (cnt.at[c], cnt.at[c]), (tok_hbm, tok.at[c]))
        )
    ]
    for copy in starts:
        copy.start()
    tok_in.wait()
    for copy in starts:
        copy.wait()

    meta[0] = cnt[...]

    def meta_copy(i, o):
        return pltpu.make_async_remote_copy(
            cnt, meta.at[i], meta_s.at[i], meta_r.at[i],
            device_id=device_at(o, 1), device_id_type=MESH,
        )

    def send_copy(i, o):
        return pltpu.make_async_remote_copy(
            send.at[i], arr.at[i], disp_s.at[i], disp_r.at[i],
            device_id=device_at(o, 1), device_id_type=MESH,
        )

    def ret_copy(i, o):
        return pltpu.make_async_remote_copy(
            arr.at[i], ret.at[i], ret_s.at[i], ret_r.at[i],
            device_id=device_at(o, -1), device_id_type=MESH,
        )

    def tell(b, carry):
        offs = offsets_of(b)
        for j in range(8):
            i = b * 8 + j

            def go(i=i, j=j):
                meta_copy(i, offs[j]).start()

            if j == 0:
                pl.when(b > 0)(go)
            else:
                go()
        return carry

    lax.fori_loop(0, 8, tell, 0)

    row_io = lax.broadcasted_iota(jnp.int32, (16, 256), 0).astype(F32)

    def aux_row(k, pair):
        return jnp.concatenate(
            [aux[0, k, pl.ds(pair, 1), :], aux[1, k, pl.ds(pair, 1), :]], axis=1
        )

    def dispatch(b, carry):
        offs = offsets_of(b)
        for j in range(8):
            pair = pair_at(offs[j])
            hit = (row_io == aux_row(0, pair)) | (row_io == aux_row(1, pair))
            onehot[16 * j : 16 * j + 16, :] = jnp.where(hit, 1.0, 0.0).astype(BF16)

        def tile(n, inner):
            cols = pl.ds(pl.multiple_of(n * CT, CT), CT)
            rows = jnp.dot(
                onehot[...], tok[:, :, cols].reshape(256, CT), preferred_element_type=F32
            )
            send[pl.ds(b * 8, 8), :, :, cols] = rows.reshape(8, 2, 8, CT).astype(BF16)
            return inner

        lax.fori_loop(0, NT, tile, 0)
        for j in range(8):
            i = b * 8 + j

            def go(i=i, j=j):
                send_copy(i, offs[j]).start()

            if j == 0:
                pl.when(b > 0)(go)
            else:
                go()
        return carry

    lax.fori_loop(0, 8, dispatch, 0)
    arr[0] = send[0]

    for copy in w_in:
        copy.wait()

    me_lane = dp * 16 + ex
    lane_io = lax.broadcasted_iota(jnp.int32, (1, 1, 1, 128), 3)
    mix_row = lax.broadcasted_iota(jnp.int32, (GS, 8, 1), 1)

    def experts(g, carry):
        chunk = pl.ds(g * GS, GS)

        def arrived(i, inner):
            @pl.when(i > 0)
            def _():
                meta_copy(i, (0, 0, 0)).wait_recv()
                send_copy(i, (0, 0, 0)).wait_recv()

            return inner

        lax.fori_loop(g * GS, g * GS + GS, arrived, 0)
        mix = pltpu.make_async_remote_copy(
            arr.at[chunk, 1], pmix.at[chunk], mix_s.at[g], mix_r.at[g],
            device_id=partner, device_id_type=MESH,
        )
        mix.start()

        def load_own(n, inner):
            cols = pl.ds(pl.multiple_of(n * CT, CT), CT)
            xs[0 : GS * 16, cols] = arr[chunk, :, :, cols].astype(F32).reshape(GS * 16, CT).astype(BF16)
            return inner

        lax.fori_loop(0, NT, load_own, 0)
        mix.wait()

        def load_mix(n, inner):
            cols = pl.ds(pl.multiple_of(n * CT, CT), CT)
            xs[GS * 16 : GS * 24, cols] = pmix[chunk, :, cols].astype(F32).reshape(GS * 8, CT).astype(BF16)
            return inner

        lax.fori_loop(0, NT, load_mix, 0)

        def hidden(n, inner):
            cols = pl.ds(pl.multiple_of(n * 256, 256), 256)
            gate = jnp.dot(xs[...], wg[:, cols], preferred_element_type=F32)
            up = jnp.dot(xs[...], wu[:, cols], preferred_element_type=F32)
            hid[:, cols] = (gate / (1.0 + jnp.exp(-gate)) * up).astype(BF16)
            return inner

        lax.fori_loop(0, FF // 256, hidden, 0)

        def down(n, inner):
            cols = pl.ds(pl.multiple_of(n * CT, CT), CT)
            rows = jnp.dot(hid[...], wd[:, cols], preferred_element_type=F32)
            arr[chunk, :, :, cols] = rows[0 : GS * 16].reshape(GS, 2, 8, CT).astype(BF16)
            pmix[chunk, :, cols] = rows[GS * 16 :].reshape(GS, 8, CT).astype(BF16)
            return inner

        lax.fori_loop(0, NT, down, 0)
        back = pltpu.make_async_remote_copy(
            pmix.at[chunk], pout.at[chunk], po_s.at[g], po_r.at[g],
            device_id=partner, device_id_type=MESH,
        )
        back.start()
        found = jnp.sum(jnp.where(lane_io == me_lane, meta[chunk], 0.0), axis=3, keepdims=True)
        own0, own1 = found[:, 0], found[:, 1]
        bound = jnp.where(mix_row < 4, own0, own1)
        mine = (4 + lax.rem(mix_row, 4)).astype(F32) < bound
        back.wait()

        def choose(n, inner):
            cols = pl.ds(pl.multiple_of(n * CT, CT), CT)
            own = arr[chunk, 1, :, cols].astype(F32)
            other = pout[chunk, :, cols].astype(F32)
            arr[chunk, 1, :, cols] = jnp.where(mine, own, other).astype(BF16)
            return inner

        lax.fori_loop(0, NT, choose, 0)
        for h in range(GS // 8):
            offs = offsets_of(g * (GS // 8) + h)
            for j in range(8):
                i = g * GS + h * 8 + j

                def go(i=i, o=offs[j]):
                    ret_copy(i, o).start()

                if h == 0 and j == 0:
                    pl.when(g > 0)(go)
                else:
                    go()
        return carry

    lax.fori_loop(0, NG, experts, 0)
    ret[0] = arr[0]
    acc[...] = jnp.zeros_like(acc)

    def combine(g, carry):
        def arrived(i, inner):
            @pl.when(i > 0)
            def _():
                ret_copy(i, (0, 0, 0)).wait_recv()

            return inner

        lax.fori_loop(g * GS, g * GS + GS, arrived, 0)
        blocks = []
        for h in range(GS // 8):
            offs = offsets_of(g * (GS // 8) + h)
            for j in range(8):
                pair = pair_at(offs[j])
                blocks.append(
                    jnp.where(row_io == aux_row(0, pair), aux_row(2, pair), 0.0)
                    + jnp.where(row_io == aux_row(1, pair), aux_row(3, pair), 0.0)
                )
        mixer = jnp.transpose(jnp.concatenate(blocks, axis=0))
        high = mixer.astype(BF16)
        comb[0:256, :] = high
        comb[256:512, :] = (mixer - high.astype(F32)).astype(BF16)

        def tile(n, inner):
            cols = pl.ds(pl.multiple_of(n * CT, CT), CT)
            rows = ret[pl.ds(g * GS, GS), :, :, cols].astype(F32).reshape(GS * 16, CT).astype(BF16)
            both = jnp.dot(comb[...], rows, preferred_element_type=F32)
            acc[:, :, cols] += (both[0:256] + both[256:512]).reshape(2, 128, CT)
            return inner

        lax.fori_loop(0, NT, tile, 0)
        return carry

    lax.fori_loop(0, NG, combine, 0)

    def part_copy(n):
        cols = pl.ds(pl.multiple_of(n * CT, CT), CT)
        return pltpu.make_async_remote_copy(
            acc.at[1 - c, :, cols], part.at[:, cols], part_s.at[n], part_r.at[n],
            device_id=partner, device_id_type=MESH,
        )

    def part_go(n, carry):
        part_copy(n).start()
        return carry

    lax.fori_loop(0, NT, part_go, 0)

    def finish(n, carry):
        cols = pl.ds(pl.multiple_of(n * CT, CT), CT)
        part_copy(n).wait_recv()
        out_ref[:, cols] = (acc[c, :, cols] + part[:, cols]).astype(BF16)
        return carry

    lax.fori_loop(0, NT, finish, 0)

    def drain(i, carry):
        meta_copy(i, (0, 0, 0)).wait_send()
        send_copy(i, (0, 0, 0)).wait_send()
        ret_copy(i, (0, 0, 0)).wait_send()
        return carry

    lax.fori_loop(1, CHIPS, drain, 0)

    def part_drain(n, carry):
        part_copy(n).wait_send()
        return carry

    lax.fori_loop(0, NT, part_drain, 0)


def local(tokens, router_weights, expert_ids, gate_weight, up_weight, down_weight):
    sem = pltpu.SemaphoreType.DMA
    hbm = pl.BlockSpec(memory_space=pl.ANY)
    vmem = pl.BlockSpec(memory_space=pltpu.VMEM)
    return pl.pallas_call(
        kernel,
        out_shape=jax.ShapeDtypeStruct((128, D), BF16),
        in_specs=[hbm, vmem, vmem, hbm, hbm, hbm],
        out_specs=vmem,
        scratch_shapes=[
            pltpu.VMEM((2, 128, D), BF16),
            pltpu.VMEM((2, 4, 64, 128), F32),
            pltpu.VMEM((4, 64, 128), F32),
            pltpu.VMEM((2, 1, 128), F32),
            pltpu.VMEM((CHIPS, 2, 1, 128), F32),
            pltpu.VMEM((128, 256), BF16),
            pltpu.VMEM((CHIPS, 2, 8, D), BF16),
            pltpu.VMEM((CHIPS, 2, 8, D), BF16),
            pltpu.VMEM((CHIPS, 8, D), BF16),
            pltpu.VMEM((CHIPS, 8, D), BF16),
            pltpu.VMEM((CHIPS, 2, 8, D), BF16),
            pltpu.VMEM((D, FF), BF16),
            pltpu.VMEM((D, FF), BF16),
            pltpu.VMEM((FF, D), BF16),
            pltpu.VMEM((GS * 24, D), BF16),
            pltpu.VMEM((GS * 24, FF), BF16),
            pltpu.VMEM((512, GS * 16), BF16),
            pltpu.VMEM((2, 128, D), F32),
            pltpu.VMEM((128, D), F32),
            sem, sem((3,)), sem((3,)), sem((3,)),
            sem((CHIPS,)), sem((CHIPS,)), sem((CHIPS,)), sem((CHIPS,)), sem((CHIPS,)), sem((CHIPS,)),
            sem((NG,)), sem((NG,)), sem((NG,)), sem((NG,)), sem((NT,)), sem((NT,)),
        ],
        compiler_params=pltpu.CompilerParams(
            collective_id=0, has_side_effects=True, vmem_limit_bytes=67043328
        ),
    )(
        tokens, expert_ids.T, router_weights.T,
        gate_weight[0], up_weight[0], down_weight[0],
    )


def solution(mesh):
    split = ("dp", "expert")
    return jax.shard_map(
        local,
        mesh=mesh,
        in_specs=(
            P(split, None), P(split, None), P(split, None),
            P(split, None, None), P(split, None, None), P(split, None, None),
        ),
        out_specs=P(split, None),
        check_vma=False,
    )
```
